32 devices in a mesh: area: 8 (over z, x), tile: 4 (over y, core).
Axes of the slice: x: 2, y: 2, z: 4, core: 2. Of those that a mesh axis runs over, the one named last changes fastest.
Arguments:
- start_rates: bfloat16 [8, 256, 4096], P('area', None, 'tile'), may hold values from -0.8984375 to 0.8984375
- stim_drive: bfloat16 [8, 256, 4096], P('area', None, 'tile'), may hold values from -6 to 6
- leak_rates: float32 [8, 4096], P('area', 'tile'), may hold values from 0.2 to 0.9
- block_weights: bfloat16 [8, 32, 20, 128, 128], P('area', 'tile'), may hold values from -0.21875 to 0.21875
- near_index: int32 [8, 32, 12], P('area', 'tile'), may hold values from 0 to 9, as said below
- far_index: int32 [8, 32, 8], P('area', 'tile'), may hold values from 0 to 7, as said below
Outputs:
- final_rates: bfloat16 [8, 256, 4096], P('area', None, 'tile')
The draws below stay inside these ranges and needn't reach their ends.
Inputs may be any that keep to these rules, and one draw needn't show every extreme that they name: `near_index`: an entry names one of the tile's own blocks (1 to 8) or the adjacent edge block of the neighbouring tile (0 the lower, 9 the upper). Slot 0 of every tile's first row block is 0 and slot 1 of every tile's last row block is 9. `far_index`: an entry q names the projecting block (the first block) of the same tile in section q, a section of another area; the areas are the consecutive groups of 3, 2, 2 and 1 eighths of the sections, in that order.
All inputs are finite; a program needn't handle non-finite values.
Results may differ from the reference program's by a relative error of at most 0.005.
Values may be sent and summed in bfloat16 or wider, within the bound.
A program may use at most 64 MiB of HBM per device.

```python
import jax
import jax.numpy as jnp
from jax import lax

BLK = 128
RB = 8
K_REC = 12
K_INT = 8
EXPORT = 1
STEPS = 3
BATCH = 256
NEURONS = 4096
N_AREA = 8
N_TILE = 4


def draw_near_index(key, part):
    row_count = N_TILE * RB
    slot_values = jax.random.randint(key, (N_AREA, row_count, K_REC), 0, RB + 2)
    within = jnp.arange(row_count) % RB
    slot_number = jnp.arange(K_REC)
    first_block = (within == 0)[None, :, None] & (slot_number == 0)[None, None, :]
    last_block = (within == RB - 1)[None, :, None] & (slot_number == 1)[None, None, :]
    slot_values = jnp.where(first_block, 0, slot_values)
    slot_values = jnp.where(last_block, RB + 1, slot_values)
    return slot_values.astype(jnp.int32)


def draw_far_index(key, part):
    unit_size = N_AREA // 8
    device_ids = jnp.arange(N_AREA)
    group_start = jnp.where(device_ids >= 7 * unit_size, 7 * unit_size, jnp.where(device_ids >= 5 * unit_size, 5 * unit_size, jnp.where(device_ids >= 3 * unit_size, 3 * unit_size, 0)))
    group_end = jnp.where(device_ids >= 7 * unit_size, 8 * unit_size, jnp.where(device_ids >= 5 * unit_size, 7 * unit_size, jnp.where(device_ids >= 3 * unit_size, 5 * unit_size, 3 * unit_size)))
    own_count = group_end - group_start
    key_device, key_export = jax.random.split(key)
    shape_all = (N_AREA, N_TILE * RB, K_INT)
    upper_bound = jnp.broadcast_to((N_AREA - own_count)[:, None, None], shape_all)
    drawn_rank = jax.random.randint(key_device, shape_all, 0, upper_bound)
    source_device = jnp.where(drawn_rank < group_start[:, None, None], drawn_rank, drawn_rank + own_count[:, None, None])
    export_pick = jax.random.randint(key_export, shape_all, 0, EXPORT)
    return (source_device * EXPORT + export_pick).astype(jnp.int32)


def level_of(stream_key, shape, pieces, smallest, high):
    def one(position, shards_of):
        heights = jax.random.uniform(jax.random.fold_in(jax.random.fold_in(stream_key, 6), position), (shards_of,), jnp.float32, smallest / len(pieces), high / len(pieces))
        return jnp.repeat(jnp.exp(heights), shape[position] // shards_of).reshape((-1,) + (1,) * (len(shape) - position - 1))

    loudness = one(*pieces[0])
    for cut in pieces[1:]:
        loudness = loudness * one(*cut)
    return loudness


def gaussian(stream_key, shape, spread, most, shards=(), kind=jnp.bfloat16):
    result = spread * jax.random.normal(stream_key, shape, jnp.float32)
    if shards:
        result = result * level_of(stream_key, shape, shards, -0.22, 0.18)
    return jnp.clip(result, -most, most).astype(kind)


def setup_inputs(seed: int = 0) -> dict:
    key_list = jax.random.split(jax.random.key(seed), 7)
    start_rates = jnp.clip(jax.random.uniform(key_list[0], (N_AREA, BATCH, NEURONS), jnp.float32, -0.8984375, 0.8984375) * level_of(key_list[0], (N_AREA, BATCH, NEURONS), ((0, 8), (2, 4)), -0.4, 0.0), -0.8984375, 0.8984375).astype(jnp.bfloat16)
    stim_drive = gaussian(key_list[1], (N_AREA, BATCH, NEURONS), 1.0, 6.0, ((0, 8), (2, 4)))
    leak_rates = jnp.clip(0.2 + 0.7 * jax.random.uniform(key_list[2], (N_AREA, NEURONS), jnp.float32) ** level_of(key_list[2], (N_AREA, NEURONS), ((0, 8), (1, 4)), -0.2, 0.2), 0.2, 0.9)
    block_weights = gaussian(key_list[3], (N_AREA, N_TILE * RB, K_REC + K_INT, BLK, BLK), ((K_REC + K_INT) * BLK // 3) ** -0.5, 0.21875, ((0, 8), (1, 4)))
    near_index = draw_near_index(jax.random.fold_in(key_list[6], 71), 0)
    far_index = draw_far_index(jax.random.fold_in(key_list[6], 71), 0)
    return dict(start_rates=start_rates, stim_drive=stim_drive, leak_rates=leak_rates, block_weights=block_weights, near_index=near_index, far_index=far_index)


def reference(start_rates, stim_drive, leak_rates, block_weights, near_index, far_index):
    block_count = N_TILE * RB
    tile_number = jnp.arange(block_count, dtype=jnp.int32) // RB
    near_column = (tile_number * RB)[None, :, None] + near_index
    far_column = (tile_number * (N_AREA * EXPORT))[None, :, None] + far_index
    rates_now = start_rates
    for step_index in range(STEPS):
        grouped = rates_now.reshape(N_AREA, BATCH, N_TILE, RB, BLK)[:, :, :, :EXPORT, :]
        export_pool = jnp.transpose(grouped, (1, 2, 0, 3, 4)).reshape(BATCH, N_TILE * N_AREA * EXPORT, BLK)

        def one_area(area_number):
            area_rates = rates_now[area_number].reshape(BATCH, block_count, BLK)
            edge_zero = jnp.zeros((BATCH, 1, BLK), jnp.bfloat16)
            padded = jnp.concatenate((edge_zero, area_rates, edge_zero), axis=1)
            near_selected = jnp.take(padded, near_column[area_number], axis=1)
            far_selected = jnp.take(export_pool, far_column[area_number], axis=1)
            selected = jnp.concatenate((near_selected, far_selected), axis=2).astype(jnp.float32)
            current = jnp.einsum("brki,rkio->bro", selected, block_weights[area_number].astype(jnp.float32))
            current = current.reshape(BATCH, -1) + stim_drive[area_number].astype(jnp.float32)
            leak_now = leak_rates[area_number]
            updated = (1.0 - leak_now) * rates_now[area_number].astype(jnp.float32) + leak_now * jnp.tanh(current)
            return updated.astype(jnp.bfloat16)

        rates_now = lax.map(one_area, jnp.arange(N_AREA, dtype=jnp.int32))
    return rates_now
```

```python
import functools

import jax
import jax.numpy as jnp
from jax import lax
from jax.experimental import pallas as pl
from jax.experimental.pallas import tpu as pltpu
from jax.sharding import PartitionSpec as P

STEPS = 3
CHUNKS = 2
PIECES = 4
LONG = 3
ORDER = (
    ("down",),
    ("high",),
    ("fetch", 0),
    ("up", 1),
    ("across",),
    ("fetch", 1),
    ("up", 2),
    ("load",),
    ("relay", 0, 0, 1),
    ("relay", 0, 0, -1),
    ("start", 0),
    ("start", 1),
    ("relay", 0, 0, 2),
    ("relay", 0, 0, -2),
    ("relay", 0, 1, 1),
    ("relay", 0, 1, -1),
    ("up", 3),
    ("start", 2),
    ("start", 3),
    ("relay", 0, 0, 3),
    ("relay", 0, 0, -3),
    ("relay", 0, 1, 2),
    ("relay", 0, 1, -2),
    ("relay", 0, 1, 3),
    ("relay", 0, 1, -3),
    ("first", 0, 0),
    ("rest", 0, 0),
    ("first", 0, 1),
    ("rest", 0, 1),
    ("relay", 1, 0, 1),
    ("relay", 1, 0, -1),
    ("relay", 1, 0, 2),
    ("relay", 1, 0, -2),
    ("relay", 1, 0, 3),
    ("relay", 1, 0, -3),
    ("near", 1, 0),
    ("relay", 1, 1, 1),
    ("relay", 1, 1, -1),
    ("relay", 1, 1, 2),
    ("relay", 1, 1, -2),
    ("relay", 1, 1, 3),
    ("relay", 1, 1, -3),
    ("near", 1, 1),
    ("first", 1, 0),
    ("rest", 1, 0),
    ("first", 1, 1),
    ("rest", 1, 1),
    ("relay", 2, 0, 1),
    ("relay", 2, 0, -1),
    ("relay", 2, 0, 2),
    ("relay", 2, 0, -2),
    ("relay", 2, 0, 3),
    ("relay", 2, 0, -3),
    ("near", 2, 0),
    ("relay", 2, 1, 1),
    ("relay", 2, 1, -1),
    ("relay", 2, 1, 2),
    ("relay", 2, 1, -2),
    ("relay", 2, 1, 3),
    ("relay", 2, 1, -3),
    ("near", 2, 1),
    ("first", 2, 0),
    ("first", 2, 1),
)
FIRST = next(step[1] for step in ORDER if step[0] == "start")
MESH = pl.DeviceIdType.MESH


def group_of(section, n_area):
    unit = n_area // 8
    return (
        (section >= 3 * unit).astype(jnp.int32)
        + (section >= 5 * unit).astype(jnp.int32)
        + (section >= 7 * unit).astype(jnp.int32)
    )


def kernel(sizes, near_hbm, far_hbm, rates_hbm, drive_hbm, leak_hbm, w_hbm, out_ref, *scratch):
    n_area, n_tile = sizes[:2]
    n_col = n_area // 2
    dma = pltpu.SemaphoreType.DMA
    regular = pltpu.SemaphoreType.REGULAR
    refs = (near_hbm, far_hbm, rates_hbm, drive_hbm, leak_hbm, w_hbm, out_ref)
    pl.run_scoped(
        functools.partial(program, sizes, refs, scratch),
        dma((9,)),
        dma((2, CHUNKS, n_area)),
        dma((CHUNKS, 2 * n_col - 1)),
        dma((CHUNKS,)),
        dma((CHUNKS, 2 * n_col - 1)),
        dma((CHUNKS, 2)),
        dma((STEPS, CHUNKS, 2)),
        regular((n_col + 2,)),
    )


def program(
    sizes, refs, scratch,
    load_sem, far_recv, col_send, own_send, relay_send, edge_send, edge_recv, in_sem,
):
    n_area, n_tile, batch, rows, k_near, k_far, blk = sizes
    near_hbm, far_hbm, rates_hbm, drive_hbm, leak_hbm, w_hbm, out_ref = refs
    n_col = n_area // 2
    part = batch // CHUNKS
    chunks = range(CHUNKS)
    near_idx, far_idx, leak_ref, drive, weights, acc, start = scratch[:7]
    rest = scratch[7:]
    nears = {
        (t, c): rest[(t - 1) * CHUNKS + c] for t in range(1, STEPS) for c in chunks
    }
    rest = rest[(STEPS - 1) * CHUNKS :]
    fars = {(t, c): rest[t * CHUNKS + c] for t in range(STEPS) for c in chunks}

    area = lax.axis_index("area")
    tile = lax.axis_index("tile")
    side = lax.rem(area, 2)
    level = area // 2
    partner = area + 1 - 2 * side
    has_low = tile > 0
    has_high = tile < n_tile - 1

    def needs(section, source):
        return group_of(section, n_area) != group_of(source, n_area)

    def column_needs(section, source):
        mate = section + 1 - 2 * lax.rem(section, 2)
        return jnp.logical_or(needs(section, source), needs(mate, source))

    near_first = [s * d for d in range(1, n_col) for s in (1, -1)]
    far_first = [s * d for d in range(n_col - 1, 0, -1) for s in (1, -1)]

    def inside(offset):
        return jnp.logical_and(level + offset >= 0, level + offset < n_col)

    def member(offset):
        return area + 2 * offset

    def span(c):
        return pl.ds(c * part, part)

    barrier = pltpu.get_barrier_semaphore()
    in_x, in_t = 0, n_col + 1

    for d in range(1, n_col):
        @pl.when(inside(d))
        def _(d=d):
            pl.semaphore_signal(barrier, inc=1, device_id=(member(d), tile), device_id_type=MESH)

    @pl.when(side == 0)
    def _():
        pl.semaphore_signal(barrier, inc=1, device_id=(partner, tile), device_id_type=MESH)

    @pl.when(has_high)
    def _():
        pl.semaphore_signal(barrier, inc=1, device_id=(area, tile + 1), device_id_type=MESH)

    def load(r, sem):
        return pltpu.make_async_copy(
            rates_hbm.at[:, pl.ds(r * blk, blk)], start.at[r + 1], load_sem.at[sem]
        )

    def load_drive(r):
        return pltpu.make_async_copy(
            drive_hbm.at[:, pl.ds(r * blk, blk)], drive.at[r], load_sem.at[2]
        )

    near_part, far_part = pl.ds(0, k_near * blk), pl.ds(k_near * blk, k_far * blk)

    def load_near_weights(r):
        return pltpu.make_async_copy(
            w_hbm.at[r, near_part], weights.at[r, near_part], load_sem.at[1]
        )

    def load_far_weights(r):
        return pltpu.make_async_copy(
            w_hbm.at[r, far_part], weights.at[r, far_part], load_sem.at[8]
        )

    load_near = pltpu.make_async_copy(near_hbm, near_idx, load_sem.at[3])
    load_far = pltpu.make_async_copy(far_hbm, far_idx, load_sem.at[4])
    load_leak = pltpu.make_async_copy(leak_hbm, leak_ref, load_sem.at[5])

    load(0, 6).start()
    load(rows - 1, 7).start()
    load_near.start()
    load_far.start()
    load_leak.start()

    def fetch(part_of):
        if part_of == 0:
            for r in range(1, rows - 1):
                load(r, 0).start()
            for r in range(rows):
                load_near_weights(r).start()
                load_drive(r).start()
        else:
            for r in range(rows):
                load_far_weights(r).start()

    below = level + side + has_low.astype(jnp.int32)

    @pl.when(below > 0)
    def _():
        pl.semaphore_wait(barrier, below)

    for d in range(1, n_col):
        @pl.when(inside(-d))
        def _(d=d):
            pl.semaphore_signal(
                in_sem.at[d], inc=1, device_id=(member(-d), tile), device_id_type=MESH
            )

    @pl.when(side == 1)
    def _():
        pl.semaphore_signal(in_sem.at[in_x], inc=1, device_id=(partner, tile), device_id_type=MESH)

    @pl.when(has_low)
    def _():
        pl.semaphore_signal(
            in_sem.at[in_t], inc=1, device_id=(area, tile - 1), device_id_type=MESH
        )

    def block_of(t, c, r):
        return start.at[r + 1, span(c)] if t == 0 else nears[t, c].at[r + 1]

    def column_copy(t, c, offset):
        return pltpu.make_async_remote_copy(
            src_ref=block_of(t, c, 0),
            dst_ref=fars[t, c].at[area],
            send_sem=col_send.at[c, offset + n_col - 1],
            recv_sem=far_recv.at[t % 2, c, area],
            device_id=(member(offset), tile),
            device_id_type=MESH,
        )

    def own_copy(t, c):
        return pltpu.make_async_remote_copy(
            src_ref=block_of(t, c, 0),
            dst_ref=fars[t, c].at[area],
            send_sem=own_send.at[c],
            recv_sem=far_recv.at[t % 2, c, area],
            device_id=(partner, tile),
            device_id_type=MESH,
        )

    def relay_copy(t, c, offset):
        source = member(offset)
        return pltpu.make_async_remote_copy(
            src_ref=fars[t, c].at[source],
            dst_ref=fars[t, c].at[source],
            send_sem=relay_send.at[c, offset + n_col - 1],
            recv_sem=far_recv.at[t % 2, c, source],
            device_id=(partner, tile),
            device_id_type=MESH,
        )

    def arrival(t, c, source):
        return pltpu.make_async_remote_copy(
            src_ref=block_of(t, c, 0),
            dst_ref=fars[t, c].at[source],
            send_sem=own_send.at[c],
            recv_sem=far_recv.at[t % 2, c, source],
            device_id=(partner, tile),
            device_id_type=MESH,
        )

    def low_copy(t, c):
        return pltpu.make_async_remote_copy(
            src_ref=start.at[1] if t == 0 else nears[t, c].at[1],
            dst_ref=start.at[rows + 1] if t == 0 else nears[t, c].at[rows + 1],
            send_sem=edge_send.at[c, 0],
            recv_sem=edge_recv.at[t, c, 1],
            device_id=(area, tile - 1),
            device_id_type=MESH,
        )

    def high_copy(t, c):
        return pltpu.make_async_remote_copy(
            src_ref=start.at[rows] if t == 0 else nears[t, c].at[rows],
            dst_ref=start.at[0] if t == 0 else nears[t, c].at[0],
            send_sem=edge_send.at[c, 1],
            recv_sem=edge_recv.at[t, c, 0],
            device_id=(area, tile + 1),
            device_id_type=MESH,
        )

    def column_step(t, c, offset, act):
        @pl.when(inside(offset))
        def _():
            @pl.when(column_needs(member(offset), area))
            def _():
                act(column_copy(t, c, offset))

    def own_step(t, c, act):
        @pl.when(needs(partner, area))
        def _():
            act(own_copy(t, c))

    def relay_step(t, c, offset, act):
        @pl.when(inside(offset))
        def _():
            @pl.when(needs(partner, member(offset)))
            def _():
                act(relay_copy(t, c, offset))

    def edge_step(t, c, low, act):
        @pl.when(has_low if low else has_high)
        def _():
            act((low_copy if low else high_copy)(t, c))

    def go(copy):
        copy.start()

    def sent(copy):
        copy.wait_send()

    def export_sent(t, c):
        for offset in far_first:
            column_step(t, c, offset, sent)
        own_step(t, c, sent)

    def send_export(t, c):
        for offset in far_first:
            column_step(t, c, offset, go)
        own_step(t, c, go)

    def edges_sent(t, c):
        edge_step(t, c, True, sent)
        edge_step(t, c, False, sent)

    def wait_edges(t, c):
        @pl.when(has_high)
        def _():
            low_copy(t, c).wait_recv()

        @pl.when(has_low)
        def _():
            high_copy(t, c).wait_recv()

    def relay(t, c, offset):
        @pl.when(inside(offset))
        def _():
            @pl.when(needs(partner, member(offset)))
            def _():
                arrival(t, c, member(offset)).wait_recv()
                if t > 0:
                    relay_copy(t - 1, c, offset).wait_send()
                relay_copy(t, c, offset).start()

    def wait_far(t, c):
        @pl.when(needs(area, partner))
        def _():
            arrival(t, c, partner).wait_recv()

        for offset in near_first:
            @pl.when(inside(offset))
            def _(offset=offset):
                column, across = member(offset), partner + 2 * offset
                direct = jnp.logical_not(needs(partner, column))

                @pl.when(jnp.logical_and(direct, needs(area, column)))
                def _():
                    arrival(t, c, column).wait_recv()

                @pl.when(needs(area, across))
                def _():
                    arrival(t, c, across).wait_recv()

    def chain(pieces, w_of):
        total = None
        for k in range(0, len(pieces), 2):
            pair = jnp.concatenate([p() for p in pieces[k : k + 2]], axis=1)
            term = jnp.dot(pair, w_of(k, pair.shape[1]), preferred_element_type=jnp.float32)
            total = term if total is None else total + term
        return total

    def near_row(buffer, r, rows_of):
        pieces = [lambda k=k: buffer[near_idx[r, k]] for k in range(k_near)]
        total = chain(pieces, lambda k, n: weights[r, pl.ds(k * blk, n), :])
        acc[r, rows_of, :] = total + drive[r, rows_of, :].astype(jnp.float32)

    def far_row(t, c, r):
        pieces = [lambda k=k: fars[t, c][far_idx[r, k]] for k in range(k_far)]
        total = chain(pieces, lambda k, n: weights[r, pl.ds((k_near + k) * blk, n), :])
        current = acc[r, span(c), :] + total
        rates = start[r + 1, span(c), :] if t == 0 else nears[t, c][r + 1]
        leak = leak_ref[r]
        value = ((1.0 - leak) * rates.astype(jnp.float32) + leak * jnp.tanh(current)).astype(
            jnp.bfloat16
        )
        if t + 1 < STEPS:
            nears[t + 1, c][r + 1] = value
        else:
            out_ref[span(c), pl.ds(pl.multiple_of(r * blk, blk), blk)] = value

    def near_start(piece):
        count = rows // PIECES
        if piece == FIRST:
            wait_edges(0, 0)

        @pl.loop(piece * count, (piece + 1) * count, unroll=count)
        def _(r):
            near_row(start, r, slice(None))

    def near_chunk(t, c):
        wait_edges(t, c)

        @pl.loop(0, rows, unroll=rows // 2)
        def _(r):
            near_row(nears[t, c], r, span(c))

    def far_first_row(t, c):
        if (t, c) == (0, 0):
            load_last()
        wait_far(t, c)
        if t + 1 == STEPS:
            @pl.loop(0, rows, unroll=rows // 2)
            def _(r):
                far_row(t, c, r)

            return
        export_sent(t, c)
        far_row(t, c, 0)
        send_export(t + 1, c)

    def far_rest(t, c):
        if t > 0 or c == 0:
            edges_sent(t, c)
        edge_step(t + 1, c, True, go)

        @pl.loop(1, rows, unroll=rows - 1)
        def _(r):
            far_row(t, c, r)

        edge_step(t + 1, c, False, go)

    def send_down():
        load(0, 6).wait()
        for c in chunks:
            for d in range(n_col - 1, 0, -1):
                column_step(0, c, -d, go)

        @pl.when(side == 1)
        def _():
            for c in chunks:
                own_step(0, c, go)

        edge_step(0, 0, True, go)

    def send_high():
        load(rows - 1, 7).wait()

        @pl.when(has_high)
        def _():
            pl.semaphore_wait(in_sem.at[in_t], 1)

        edge_step(0, 0, False, go)

    def send_across():
        @pl.when(side == 0)
        def _():
            pl.semaphore_wait(in_sem.at[in_x], 1)
            for c in chunks:
                own_step(0, c, go)

    def send_up(d):
        @pl.when(inside(d))
        def _():
            pl.semaphore_wait(in_sem.at[d], 1)

        for c in chunks:
            column_step(0, c, d, go)

    def load_rest():
        zeros = jnp.zeros((part, blk), jnp.bfloat16)

        @pl.when(jnp.logical_not(has_low))
        def _():
            start[0] = jnp.zeros((batch, blk), jnp.bfloat16)
            for key in nears:
                nears[key][0] = zeros

        @pl.when(jnp.logical_not(has_high))
        def _():
            start[rows + 1] = jnp.zeros((batch, blk), jnp.bfloat16)
            for key in nears:
                nears[key][rows + 1] = zeros

        inner = start.at[pl.ds(2, rows - 2)]
        pltpu.make_async_copy(inner, inner, load_sem.at[0]).wait()
        load_near.wait()
        near_weights = weights.at[:, near_part]
        pltpu.make_async_copy(near_weights, near_weights, load_sem.at[1]).wait()
        pltpu.make_async_copy(drive, drive, load_sem.at[2]).wait()

    def load_last():
        far_weights = weights.at[:, far_part]
        pltpu.make_async_copy(far_weights, far_weights, load_sem.at[8]).wait()
        load_far.wait()
        load_leak.wait()

    steps = {
        "down": send_down,
        "across": send_across,
        "high": send_high,
        "up": send_up,
        "load": load_rest,
        "fetch": fetch,
        "start": near_start,
        "first": far_first_row,
        "rest": far_rest,
        "near": near_chunk,
    }
    for name, *at in ORDER:
        if name == "up" and at[0] >= LONG:
            for d in range(LONG, n_col):
                send_up(d)
        elif name == "up":
            if at[0] < n_col:
                send_up(*at)
        elif name == "relay":
            t, c, offset = at
            away = abs(offset)
            if away >= LONG:
                for d in range(LONG, n_col):
                    relay(t, c, d if offset > 0 else -d)
            elif away < n_col:
                relay(t, c, offset)
        else:
            steps[name](*at)

    t = STEPS - 1
    for c in chunks:
        export_sent(t, c)
        for offset in near_first:
            relay_step(t, c, offset, sent)
        edges_sent(t, c)


def body(n_area, n_tile, start_rates, stim_drive, leak_rates, block_weights, near_index, far_index):
    _, batch, width = start_rates.shape
    _, rows, slots, blk, _ = block_weights.shape
    k_near, k_far = near_index.shape[-1], far_index.shape[-1]
    sizes = (n_area, n_tile, batch, rows, k_near, k_far, blk)
    part = batch // CHUNKS
    any_spec = pl.BlockSpec(memory_space=pl.ANY)
    vmem_spec = pl.BlockSpec(memory_space=pltpu.VMEM)
    scratch = (
        [
            pltpu.SMEM((rows, k_near), jnp.int32),
            pltpu.SMEM((rows, k_far), jnp.int32),
            pltpu.VMEM((rows, 1, blk), jnp.float32),
            pltpu.VMEM((rows, batch, blk), jnp.bfloat16),
            pltpu.VMEM((rows, slots * blk, blk), jnp.bfloat16),
            pltpu.VMEM((rows, batch, blk), jnp.float32),
            pltpu.VMEM((rows + 2, batch, blk), jnp.bfloat16),
        ]
        + [pltpu.VMEM((rows + 2, part, blk), jnp.bfloat16) for _ in range((STEPS - 1) * CHUNKS)]
        + [pltpu.VMEM((n_area, part, blk), jnp.bfloat16) for _ in range(STEPS * CHUNKS)]
    )
    out = pl.pallas_call(
        functools.partial(kernel, sizes),
        out_shape=pltpu.MemorySpace.VMEM((batch, width), jnp.bfloat16),
        in_specs=[any_spec] * 6,
        out_specs=vmem_spec,
        scratch_shapes=scratch,
        compiler_params=pltpu.CompilerParams(
            collective_id=0, has_side_effects=True, vmem_limit_bytes=56 * 1024 * 1024
        ),
        name="rate_steps",
    )(
        near_index[0],
        far_index[0],
        start_rates[0],
        stim_drive[0],
        leak_rates[0].reshape(rows, 1, blk),
        block_weights[0].reshape(rows, slots * blk, blk),
    )
    return out[None]


def solution(mesh):
    in_specs = (
        P("area", None, "tile"),
        P("area", None, "tile"),
        P("area", "tile"),
        P("area", "tile", None, None, None),
        P("area", "tile", None),
        P("area", "tile", None),
    )
    out_specs = P("area", None, "tile")
    local = functools.partial(body, mesh.shape["area"], mesh.shape["tile"])
    return jax.shard_map(local, mesh=mesh, in_specs=in_specs, out_specs=out_specs, check_vma=False)
```

```python
import functools

import jax
import jax.numpy as jnp
from jax import lax
from jax.experimental import pallas as pl
from jax.experimental.pallas import tpu as pltpu
from jax.sharding import PartitionSpec as P

STEPS = 3
CHUNKS = 2
PIECES = 4
LONG = 3
ORDER = (
    ("down",), ("high",), ("fetch", 0), ("up", 1), ("across",), ("fetch", 1), ("up", 2),
    ("load",), ("start", 0), ("start", 1), ("up", 3), ("start", 2), ("late", 1),
    ("relay", 0, 0, 1), ("relay", 0, 0, -1), ("relay", 0, 0, 2), ("relay", 0, 0, -2),
    ("start", 3), ("relay", 0, 0, 3), ("relay", 0, 0, -3), ("relay", 0, 1, 1),
    ("relay", 0, 1, -1), ("relay", 0, 1, 2), ("relay", 0, 1, -2), ("relay", 0, 1, 3),
    ("relay", 0, 1, -3), ("first", 0, 0), ("rest", 0, 0), ("first", 0, 1), ("rest", 0, 1),
    ("relay", 1, 0, 1), ("relay", 1, 0, -1), ("relay", 1, 0, 2), ("relay", 1, 0, -2),
    ("relay", 1, 0, 3), ("relay", 1, 0, -3), ("near", 1, 0), ("relay", 1, 1, 1),
    ("relay", 1, 1, -1), ("relay", 1, 1, 2), ("relay", 1, 1, -2), ("relay", 1, 1, 3),
    ("relay", 1, 1, -3), ("first", 1, 0), ("rest", 1, 0), ("near", 1, 1), ("first", 1, 1),
    ("rest", 1, 1), ("relay", 2, 0, 1), ("relay", 2, 0, -1), ("relay", 2, 0, 2),
    ("relay", 2, 0, -2), ("relay", 2, 0, 3), ("relay", 2, 0, -3), ("near", 2, 0),
    ("relay", 2, 1, 1), ("relay", 2, 1, -1), ("relay", 2, 1, 2), ("relay", 2, 1, -2),
    ("relay", 2, 1, 3), ("relay", 2, 1, -3), ("first", 2, 0), ("near", 2, 1), ("first", 2, 1),
)
FIRST = next(step[1] for step in ORDER if step[0] == "start")
MESH = pl.DeviceIdType.MESH


def group_of(section, n_area):
    unit = n_area // 8
    return (
        (section >= 3 * unit).astype(jnp.int32)
        + (section >= 5 * unit).astype(jnp.int32)
        + (section >= 7 * unit).astype(jnp.int32)
    )


def kernel(sizes, near_hbm, far_hbm, rates_hbm, drive_hbm, leak_hbm, w_hbm, out_ref, *scratch):
    n_area, n_tile = sizes[:2]
    n_col = n_area // 2
    dma = pltpu.SemaphoreType.DMA
    regular = pltpu.SemaphoreType.REGULAR
    refs = (near_hbm, far_hbm, rates_hbm, drive_hbm, leak_hbm, w_hbm, out_ref)
    pl.run_scoped(
        functools.partial(program, sizes, refs, scratch),
        dma((9,)),
        dma((2, CHUNKS, n_area)),
        dma((CHUNKS, 2 * n_col - 1)),
        dma((CHUNKS,)),
        dma((CHUNKS, 2 * n_col - 1)),
        dma((CHUNKS, 2)),
        dma((STEPS, CHUNKS, 2)),
        regular((n_col + 2,)),
    )


def program(
    sizes, refs, scratch,
    load_sem, far_recv, col_send, own_send, relay_send, edge_send, edge_recv, in_sem,
):
    n_area, n_tile, batch, rows, k_near, k_far, blk = sizes
    near_hbm, far_hbm, rates_hbm, drive_hbm, leak_hbm, w_hbm, out_ref = refs
    n_col = n_area // 2
    part = batch // CHUNKS
    chunks = range(CHUNKS)
    near_idx, far_idx, leak_ref, drive, weights, acc, start = scratch[:7]
    rest = scratch[7:]
    nears = {
        (t, c): rest[(t - 1) * CHUNKS + c] for t in range(1, STEPS) for c in chunks
    }
    rest = rest[(STEPS - 1) * CHUNKS :]
    fars = {(t, c): rest[t * CHUNKS + c] for t in range(STEPS) for c in chunks}

    area = lax.axis_index("area")
    tile = lax.axis_index("tile")
    side = lax.rem(area, 2)
    level = area // 2
    partner = area + 1 - 2 * side
    has_low = tile > 0
    has_high = tile < n_tile - 1

    def needs(section, source):
        return group_of(section, n_area) != group_of(source, n_area)

    def column_needs(section, source):
        mate = section + 1 - 2 * lax.rem(section, 2)
        return jnp.logical_or(needs(section, source), needs(mate, source))

    near_first = [s * d for d in range(1, n_col) for s in (1, -1)]
    far_first = [s * d for d in range(n_col - 1, 0, -1) for s in (1, -1)]

    def inside(offset):
        return jnp.logical_and(level + offset >= 0, level + offset < n_col)

    def member(offset):
        return area + 2 * offset

    def span(c):
        return pl.ds(c * part, part)

    barrier = pltpu.get_barrier_semaphore()
    in_x, in_t = 0, n_col + 1

    for d in range(1, n_col):
        @pl.when(inside(d))
        def _(d=d):
            pl.semaphore_signal(barrier, inc=1, device_id=(member(d), tile), device_id_type=MESH)

    @pl.when(side == 0)
    def _():
        pl.semaphore_signal(barrier, inc=1, device_id=(partner, tile), device_id_type=MESH)

    @pl.when(has_high)
    def _():
        pl.semaphore_signal(barrier, inc=1, device_id=(area, tile + 1), device_id_type=MESH)

    def load(r, sem):
        return pltpu.make_async_copy(
            rates_hbm.at[:, pl.ds(r * blk, blk)], start.at[r + 1], load_sem.at[sem]
        )

    def load_drive(r):
        return pltpu.make_async_copy(
            drive_hbm.at[:, pl.ds(r * blk, blk)], drive.at[r], load_sem.at[2]
        )

    near_part, far_part = pl.ds(0, k_near * blk), pl.ds(k_near * blk, k_far * blk)

    def load_near_weights(r):
        return pltpu.make_async_copy(
            w_hbm.at[r, near_part], weights.at[r, near_part], load_sem.at[1]
        )

    def load_far_weights(r):
        return pltpu.make_async_copy(
            w_hbm.at[r, far_part], weights.at[r, far_part], load_sem.at[8]
        )

    load_near = pltpu.make_async_copy(near_hbm, near_idx, load_sem.at[3])
    load_far = pltpu.make_async_copy(far_hbm, far_idx, load_sem.at[4])
    load_leak = pltpu.make_async_copy(leak_hbm, leak_ref, load_sem.at[5])

    load(0, 6).start()
    load(rows - 1, 7).start()
    load_near.start()
    load_far.start()
    load_leak.start()

    def fetch(part_of):
        if part_of == 0:
            for r in range(1, rows - 1):
                load(r, 0).start()
            for r in range(rows):
                load_near_weights(r).start()
                load_drive(r).start()
        else:
            for r in range(rows):
                load_far_weights(r).start()

    below = level + side + has_low.astype(jnp.int32)

    @pl.when(below > 0)
    def _():
        pl.semaphore_wait(barrier, below)

    for d in range(1, n_col):
        @pl.when(inside(-d))
        def _(d=d):
            pl.semaphore_signal(
                in_sem.at[d], inc=1, device_id=(member(-d), tile), device_id_type=MESH
            )

    @pl.when(side == 1)
    def _():
        pl.semaphore_signal(in_sem.at[in_x], inc=1, device_id=(partner, tile), device_id_type=MESH)

    @pl.when(has_low)
    def _():
        pl.semaphore_signal(
            in_sem.at[in_t], inc=1, device_id=(area, tile - 1), device_id_type=MESH
        )

    def block_of(t, c, r):
        return start.at[r + 1, span(c)] if t == 0 else nears[t, c].at[r + 1]

    def column_copy(t, c, offset):
        return pltpu.make_async_remote_copy(
            src_ref=block_of(t, c, 0),
            dst_ref=fars[t, c].at[area],
            send_sem=col_send.at[c, offset + n_col - 1],
            recv_sem=far_recv.at[t % 2, c, area],
            device_id=(member(offset), tile),
            device_id_type=MESH,
        )

    def own_copy(t, c):
        return pltpu.make_async_remote_copy(
            src_ref=block_of(t, c, 0),
            dst_ref=fars[t, c].at[area],
            send_sem=own_send.at[c],
            recv_sem=far_recv.at[t % 2, c, area],
            device_id=(partner, tile),
            device_id_type=MESH,
        )

    def relay_copy(t, c, offset):
        source = member(offset)
        return pltpu.make_async_remote_copy(
            src_ref=fars[t, c].at[source],
            dst_ref=fars[t, c].at[source],
            send_sem=relay_send.at[c, offset + n_col - 1],
            recv_sem=far_recv.at[t % 2, c, source],
            device_id=(partner, tile),
            device_id_type=MESH,
        )

    def arrival(t, c, source):
        return pltpu.make_async_remote_copy(
            src_ref=block_of(t, c, 0),
            dst_ref=fars[t, c].at[source],
            send_sem=own_send.at[c],
            recv_sem=far_recv.at[t % 2, c, source],
            device_id=(partner, tile),
            device_id_type=MESH,
        )

    def low_copy(t, c):
        return pltpu.make_async_remote_copy(
            src_ref=start.at[1] if t == 0 else nears[t, c].at[1],
            dst_ref=start.at[rows + 1] if t == 0 else nears[t, c].at[rows + 1],
            send_sem=edge_send.at[c, 0],
            recv_sem=edge_recv.at[t, c, 1],
            device_id=(area, tile - 1),
            device_id_type=MESH,
        )

    def high_copy(t, c):
        return pltpu.make_async_remote_copy(
            src_ref=start.at[rows] if t == 0 else nears[t, c].at[rows],
            dst_ref=start.at[0] if t == 0 else nears[t, c].at[0],
            send_sem=edge_send.at[c, 1],
            recv_sem=edge_recv.at[t, c, 0],
            device_id=(area, tile + 1),
            device_id_type=MESH,
        )

    def column_step(t, c, offset, act):
        @pl.when(inside(offset))
        def _():
            @pl.when(column_needs(member(offset), area))
            def _():
                act(column_copy(t, c, offset))

    def own_step(t, c, act):
        @pl.when(needs(partner, area))
        def _():
            act(own_copy(t, c))

    def relay_step(t, c, offset, act):
        @pl.when(inside(offset))
        def _():
            @pl.when(needs(partner, member(offset)))
            def _():
                act(relay_copy(t, c, offset))

    def edge_step(t, c, low, act):
        @pl.when(has_low if low else has_high)
        def _():
            act((low_copy if low else high_copy)(t, c))

    def go(copy):
        copy.start()

    def sent(copy):
        copy.wait_send()

    def export_sent(t, c):
        for offset in far_first:
            column_step(t, c, offset, sent)
        own_step(t, c, sent)

    def send_export(t, c):
        for offset in far_first:
            column_step(t, c, offset, go)
        own_step(t, c, go)

    def edges_sent(t, c):
        edge_step(t, c, True, sent)
        edge_step(t, c, False, sent)

    def wait_edges(t, c):
        @pl.when(has_high)
        def _():
            low_copy(t, c).wait_recv()

        @pl.when(has_low)
        def _():
            high_copy(t, c).wait_recv()

    def relay(t, c, offset):
        @pl.when(inside(offset))
        def _():
            @pl.when(needs(partner, member(offset)))
            def _():
                arrival(t, c, member(offset)).wait_recv()
                if t > 0:
                    relay_copy(t - 1, c, offset).wait_send()
                relay_copy(t, c, offset).start()

    def wait_far(t, c):
        @pl.when(needs(area, partner))
        def _():
            arrival(t, c, partner).wait_recv()

        for offset in near_first:
            @pl.when(inside(offset))
            def _(offset=offset):
                column, across = member(offset), partner + 2 * offset
                direct = jnp.logical_not(needs(partner, column))

                @pl.when(jnp.logical_and(direct, needs(area, column)))
                def _():
                    arrival(t, c, column).wait_recv()

                @pl.when(needs(area, across))
                def _():
                    arrival(t, c, across).wait_recv()

    def chain(pieces, w_of):
        total = None
        for k in range(0, len(pieces), 2):
            pair = jnp.concatenate([p() for p in pieces[k : k + 2]], axis=1)
            term = jnp.dot(pair, w_of(k, pair.shape[1]), preferred_element_type=jnp.float32)
            total = term if total is None else total + term
        return total

    def near_row(buffer, r, rows_of):
        pieces = [lambda k=k: buffer[near_idx[r, k]] for k in range(k_near)]
        total = chain(pieces, lambda k, n: weights[r, pl.ds(k * blk, n), :])
        acc[r, rows_of, :] = total + drive[r, rows_of, :].astype(jnp.float32)

    def far_row(t, c, r):
        pieces = [lambda k=k: fars[t, c][far_idx[r, k]] for k in range(k_far)]
        total = chain(pieces, lambda k, n: weights[r, pl.ds((k_near + k) * blk, n), :])
        current = acc[r, span(c), :] + total
        rates = start[r + 1, span(c), :] if t == 0 else nears[t, c][r + 1]
        leak = leak_ref[r]
        value = ((1.0 - leak) * rates.astype(jnp.float32) + leak * jnp.tanh(current)).astype(
            jnp.bfloat16
        )
        if t + 1 < STEPS:
            nears[t + 1, c][r + 1] = value
        else:
            out_ref[span(c), pl.ds(pl.multiple_of(r * blk, blk), blk)] = value

    def near_start(piece):
        count = rows // PIECES
        if piece == FIRST:
            wait_edges(0, 0)

        @pl.loop(piece * count, (piece + 1) * count, unroll=count)
        def _(r):
            near_row(start, r, slice(None))

    def near_chunk(t, c):
        wait_edges(t, c)

        @pl.loop(0, rows, unroll=rows // 2)
        def _(r):
            near_row(nears[t, c], r, span(c))

    def far_first_row(t, c):
        if (t, c) == (0, 0):
            load_last()
        wait_far(t, c)
        if t + 1 == STEPS:
            @pl.loop(0, rows, unroll=rows // 2)
            def _(r):
                far_row(t, c, r)

            return
        export_sent(t, c)
        far_row(t, c, 0)
        send_export(t + 1, c)

    def far_rest(t, c):
        if t > 0 or c == 0:
            edges_sent(t, c)
        edge_step(t + 1, c, True, go)

        @pl.loop(1, rows, unroll=rows - 1)
        def _(r):
            far_row(t, c, r)

        edge_step(t + 1, c, False, go)

    def send_down():
        load(0, 6).wait()
        for d in range(n_col - 1, 0, -1):
            column_step(0, 0, -d, go)

        @pl.when(side == 1)
        def _():
            own_step(0, 0, go)

        edge_step(0, 0, True, go)

    def send_high():
        load(rows - 1, 7).wait()

        @pl.when(has_high)
        def _():
            pl.semaphore_wait(in_sem.at[in_t], 1)

        edge_step(0, 0, False, go)

    def send_across():
        @pl.when(side == 0)
        def _():
            pl.semaphore_wait(in_sem.at[in_x], 1)
            own_step(0, 0, go)

    def send_up(d):
        @pl.when(inside(d))
        def _():
            pl.semaphore_wait(in_sem.at[d], 1)

        column_step(0, 0, d, go)

    def send_late(c):
        for offset in far_first:
            column_step(0, c, offset, go)
        own_step(0, c, go)

    def load_rest():
        zeros = jnp.zeros((part, blk), jnp.bfloat16)

        @pl.when(jnp.logical_not(has_low))
        def _():
            start[0] = jnp.zeros((batch, blk), jnp.bfloat16)
            for key in nears:
                nears[key][0] = zeros

        @pl.when(jnp.logical_not(has_high))
        def _():
            start[rows + 1] = jnp.zeros((batch, blk), jnp.bfloat16)
            for key in nears:
                nears[key][rows + 1] = zeros

        inner = start.at[pl.ds(2, rows - 2)]
        pltpu.make_async_copy(inner, inner, load_sem.at[0]).wait()
        load_near.wait()
        near_weights = weights.at[:, near_part]
        pltpu.make_async_copy(near_weights, near_weights, load_sem.at[1]).wait()
        pltpu.make_async_copy(drive, drive, load_sem.at[2]).wait()

    def load_last():
        far_weights = weights.at[:, far_part]
        pltpu.make_async_copy(far_weights, far_weights, load_sem.at[8]).wait()
        load_far.wait()
        load_leak.wait()

    steps = {
        "down": send_down,
        "across": send_across,
        "high": send_high,
        "up": send_up,
        "load": load_rest,
        "fetch": fetch,
        "late": send_late,
        "start": near_start,
        "first": far_first_row,
        "rest": far_rest,
        "near": near_chunk,
    }
    for name, *at in ORDER:
        if name == "up" and at[0] >= LONG:
            for d in range(LONG, n_col):
                send_up(d)
        elif name == "up":
            if at[0] < n_col:
                send_up(*at)
        elif name == "relay":
            t, c, offset = at
            away = abs(offset)
            if away >= LONG:
                for d in range(LONG, n_col):
                    relay(t, c, d if offset > 0 else -d)
            elif away < n_col:
                relay(t, c, offset)
        else:
            steps[name](*at)

    t = STEPS - 1
    for c in chunks:
        export_sent(t, c)
        for offset in near_first:
            relay_step(t, c, offset, sent)
        edges_sent(t, c)


def body(n_area, n_tile, start_rates, stim_drive, leak_rates, block_weights, near_index, far_index):
    _, batch, width = start_rates.shape
    _, rows, slots, blk, _ = block_weights.shape
    k_near, k_far = near_index.shape[-1], far_index.shape[-1]
    sizes = (n_area, n_tile, batch, rows, k_near, k_far, blk)
    part = batch // CHUNKS
    any_spec = pl.BlockSpec(memory_space=pl.ANY)
    vmem_spec = pl.BlockSpec(memory_space=pltpu.VMEM)
    scratch = (
        [
            pltpu.SMEM((rows, k_near), jnp.int32),
            pltpu.SMEM((rows, k_far), jnp.int32),
            pltpu.VMEM((rows, 1, blk), jnp.float32),
            pltpu.VMEM((rows, batch, blk), jnp.bfloat16),
            pltpu.VMEM((rows, slots * blk, blk), jnp.bfloat16),
            pltpu.VMEM((rows, batch, blk), jnp.float32),
            pltpu.VMEM((rows + 2, batch, blk), jnp.bfloat16),
        ]
        + [pltpu.VMEM((rows + 2, part, blk), jnp.bfloat16) for _ in range((STEPS - 1) * CHUNKS)]
        + [pltpu.VMEM((n_area, part, blk), jnp.bfloat16) for _ in range(STEPS * CHUNKS)]
    )
    out = pl.pallas_call(
        functools.partial(kernel, sizes),
        out_shape=pltpu.MemorySpace.VMEM((batch, width), jnp.bfloat16),
        in_specs=[any_spec] * 6,
        out_specs=vmem_spec,
        scratch_shapes=scratch,
        compiler_params=pltpu.CompilerParams(
            collective_id=0, has_side_effects=True, vmem_limit_bytes=56 * 1024 * 1024
        ),
        name="rate_steps",
    )(
        near_index[0],
        far_index[0],
        start_rates[0],
        stim_drive[0],
        leak_rates[0].reshape(rows, 1, blk),
        block_weights[0].reshape(rows, slots * blk, blk),
    )
    return out[None]


def solution(mesh):
    in_specs = (
        P("area", None, "tile"),
        P("area", None, "tile"),
        P("area", "tile"),
        P("area", "tile", None, None, None),
        P("area", "tile", None),
        P("area", "tile", None),
    )
    out_specs = P("area", None, "tile")
    local = functools.partial(body, mesh.shape["area"], mesh.shape["tile"])
    return jax.shard_map(local, mesh=mesh, in_specs=in_specs, out_specs=out_specs, check_vma=False)
```

```python
import functools

import jax
import jax.numpy as jnp
from jax import lax
from jax.experimental import pallas as pl
from jax.experimental.pallas import tpu as pltpu
from jax.sharding import PartitionSpec as P

STEPS = 3
CHUNKS = 2
PIECES = 4
LONG = 3
ORDER = (
    ("down",), ("high",), ("fetch", 0), ("up", 1), ("across",), ("fetch", 1), ("up", 2),
    ("load",), ("start", 0), ("up", 3), ("late", 1), ("start", 1), ("start", 2),
    ("relay", 0, 0, 1), ("relay", 0, 0, -1), ("relay", 0, 0, 2), ("relay", 0, 0, -2),
    ("start", 3), ("relay", 0, 0, 3), ("relay", 0, 0, -3), ("relay", 0, 1, 1),
    ("relay", 0, 1, -1), ("relay", 0, 1, 2), ("relay", 0, 1, -2), ("relay", 0, 1, 3),
    ("relay", 0, 1, -3), ("first", 0, 0), ("rest", 0, 0), ("first", 0, 1), ("relay", 1, 0, 1),
    ("relay", 1, 0, -1), ("rest", 0, 1), ("relay", 1, 0, 2), ("relay", 1, 0, -2),
    ("relay", 1, 0, 3), ("relay", 1, 0, -3), ("near", 1, 0), ("relay", 1, 1, 1),
    ("relay", 1, 1, -1), ("relay", 1, 1, 2), ("relay", 1, 1, -2), ("relay", 1, 1, 3),
    ("relay", 1, 1, -3), ("first", 1, 0), ("rest", 1, 0), ("near", 1, 1), ("first", 1, 1),
    ("relay", 2, 0, 1), ("relay", 2, 0, -1), ("rest", 1, 1), ("relay", 2, 0, 2),
    ("relay", 2, 0, -2), ("relay", 2, 0, 3), ("relay", 2, 0, -3), ("near", 2, 0),
    ("relay", 2, 1, 1), ("relay", 2, 1, -1), ("relay", 2, 1, 2), ("relay", 2, 1, -2),
    ("relay", 2, 1, 3), ("relay", 2, 1, -3), ("near", 2, 1), ("first", 2, 0), ("first", 2, 1),
)
FIRST = next(step[1] for step in ORDER if step[0] == "start")
MESH = pl.DeviceIdType.MESH


def group_of(section, n_area):
    unit = n_area // 8
    return (
        (section >= 3 * unit).astype(jnp.int32)
        + (section >= 5 * unit).astype(jnp.int32)
        + (section >= 7 * unit).astype(jnp.int32)
    )


def kernel(sizes, near_hbm, far_hbm, rates_hbm, drive_hbm, leak_hbm, w_hbm, out_ref, *scratch):
    n_area, n_tile = sizes[:2]
    n_col = n_area // 2
    dma = pltpu.SemaphoreType.DMA
    regular = pltpu.SemaphoreType.REGULAR
    refs = (near_hbm, far_hbm, rates_hbm, drive_hbm, leak_hbm, w_hbm, out_ref)
    pl.run_scoped(
        functools.partial(program, sizes, refs, scratch),
        dma((9,)),
        dma((2, CHUNKS, n_area)),
        dma((CHUNKS, 2 * n_col - 1)),
        dma((CHUNKS,)),
        dma((CHUNKS, 2 * n_col - 1)),
        dma((CHUNKS, 2)),
        dma((STEPS, CHUNKS, 2)),
        regular((n_col + 2,)),
    )


def program(
    sizes, refs, scratch,
    load_sem, far_recv, col_send, own_send, relay_send, edge_send, edge_recv, in_sem,
):
    n_area, n_tile, batch, rows, k_near, k_far, blk = sizes
    near_hbm, far_hbm, rates_hbm, drive_hbm, leak_hbm, w_hbm, out_ref = refs
    n_col = n_area // 2
    part = batch // CHUNKS
    chunks = range(CHUNKS)
    near_idx, far_idx, leak_ref, drive, weights, acc, start = scratch[:7]
    rest = scratch[7:]
    nears = {
        (t, c): rest[(t - 1) * CHUNKS + c] for t in range(1, STEPS) for c in chunks
    }
    rest = rest[(STEPS - 1) * CHUNKS :]
    fars = {(t, c): rest[t * CHUNKS + c] for t in range(STEPS) for c in chunks}

    area = lax.axis_index("area")
    tile = lax.axis_index("tile")
    side = lax.rem(area, 2)
    level = area // 2
    partner = area + 1 - 2 * side
    has_low = tile > 0
    has_high = tile < n_tile - 1

    def needs(section, source):
        return group_of(section, n_area) != group_of(source, n_area)

    def column_needs(section, source):
        mate = section + 1 - 2 * lax.rem(section, 2)
        return jnp.logical_or(needs(section, source), needs(mate, source))

    near_first = [s * d for d in range(1, n_col) for s in (1, -1)]
    far_first = [s * d for d in range(n_col - 1, 0, -1) for s in (1, -1)]

    def inside(offset):
        return jnp.logical_and(level + offset >= 0, level + offset < n_col)

    def member(offset):
        return area + 2 * offset

    def span(c):
        return pl.ds(c * part, part)

    barrier = pltpu.get_barrier_semaphore()
    in_x, in_t = 0, n_col + 1

    for d in range(1, n_col):
        @pl.when(inside(d))
        def _(d=d):
            pl.semaphore_signal(barrier, inc=1, device_id=(member(d), tile), device_id_type=MESH)

    @pl.when(side == 0)
    def _():
        pl.semaphore_signal(barrier, inc=1, device_id=(partner, tile), device_id_type=MESH)

    @pl.when(has_high)
    def _():
        pl.semaphore_signal(barrier, inc=1, device_id=(area, tile + 1), device_id_type=MESH)

    def load(r, sem):
        return pltpu.make_async_copy(
            rates_hbm.at[:, pl.ds(r * blk, blk)], start.at[r + 1], load_sem.at[sem]
        )

    def load_drive(r):
        return pltpu.make_async_copy(
            drive_hbm.at[:, pl.ds(r * blk, blk)], drive.at[r], load_sem.at[2]
        )

    near_part, far_part = pl.ds(0, k_near * blk), pl.ds(k_near * blk, k_far * blk)

    def load_near_weights(r):
        return pltpu.make_async_copy(
            w_hbm.at[r, near_part], weights.at[r, near_part], load_sem.at[1]
        )

    def load_far_weights(r):
        return pltpu.make_async_copy(
            w_hbm.at[r, far_part], weights.at[r, far_part], load_sem.at[8]
        )

    load_near = pltpu.make_async_copy(near_hbm, near_idx, load_sem.at[3])
    load_far = pltpu.make_async_copy(far_hbm, far_idx, load_sem.at[4])
    load_leak = pltpu.make_async_copy(leak_hbm, leak_ref, load_sem.at[5])

    load(0, 6).start()
    load(rows - 1, 7).start()
    load_near.start()
    load_far.start()
    load_leak.start()

    def fetch(part_of):
        if part_of == 0:
            for r in range(1, rows - 1):
                load(r, 0).start()
            for r in range(rows):
                load_near_weights(r).start()
                load_drive(r).start()
        else:
            for r in range(rows):
                load_far_weights(r).start()

    below = level + side + has_low.astype(jnp.int32)

    @pl.when(below > 0)
    def _():
        pl.semaphore_wait(barrier, below)

    for d in range(1, n_col):
        @pl.when(inside(-d))
        def _(d=d):
            pl.semaphore_signal(
                in_sem.at[d], inc=1, device_id=(member(-d), tile), device_id_type=MESH
            )

    @pl.when(side == 1)
    def _():
        pl.semaphore_signal(in_sem.at[in_x], inc=1, device_id=(partner, tile), device_id_type=MESH)

    @pl.when(has_low)
    def _():
        pl.semaphore_signal(
            in_sem.at[in_t], inc=1, device_id=(area, tile - 1), device_id_type=MESH
        )

    def block_of(t, c, r):
        return start.at[r + 1, span(c)] if t == 0 else nears[t, c].at[r + 1]

    def column_copy(t, c, offset):
        return pltpu.make_async_remote_copy(
            src_ref=block_of(t, c, 0),
            dst_ref=fars[t, c].at[area],
            send_sem=col_send.at[c, offset + n_col - 1],
            recv_sem=far_recv.at[t % 2, c, area],
            device_id=(member(offset), tile),
            device_id_type=MESH,
        )

    def own_copy(t, c):
        return pltpu.make_async_remote_copy(
            src_ref=block_of(t, c, 0),
            dst_ref=fars[t, c].at[area],
            send_sem=own_send.at[c],
            recv_sem=far_recv.at[t % 2, c, area],
            device_id=(partner, tile),
            device_id_type=MESH,
        )

    def relay_copy(t, c, offset):
        source = member(offset)
        return pltpu.make_async_remote_copy(
            src_ref=fars[t, c].at[source],
            dst_ref=fars[t, c].at[source],
            send_sem=relay_send.at[c, offset + n_col - 1],
            recv_sem=far_recv.at[t % 2, c, source],
            device_id=(partner, tile),
            device_id_type=MESH,
        )

    def arrival(t, c, source):
        return pltpu.make_async_remote_copy(
            src_ref=block_of(t, c, 0),
            dst_ref=fars[t, c].at[source],
            send_sem=own_send.at[c],
            recv_sem=far_recv.at[t % 2, c, source],
            device_id=(partner, tile),
            device_id_type=MESH,
        )

    def low_copy(t, c):
        return pltpu.make_async_remote_copy(
            src_ref=start.at[1] if t == 0 else nears[t, c].at[1],
            dst_ref=start.at[rows + 1] if t == 0 else nears[t, c].at[rows + 1],
            send_sem=edge_send.at[c, 0],
            recv_sem=edge_recv.at[t, c, 1],
            device_id=(area, tile - 1),
            device_id_type=MESH,
        )

    def high_copy(t, c):
        return pltpu.make_async_remote_copy(
            src_ref=start.at[rows] if t == 0 else nears[t, c].at[rows],
            dst_ref=start.at[0] if t == 0 else nears[t, c].at[0],
            send_sem=edge_send.at[c, 1],
            recv_sem=edge_recv.at[t, c, 0],
            device_id=(area, tile + 1),
            device_id_type=MESH,
        )

    def column_step(t, c, offset, act):
        @pl.when(inside(offset))
        def _():
            @pl.when(column_needs(member(offset), area))
            def _():
                act(column_copy(t, c, offset))

    def own_step(t, c, act):
        @pl.when(needs(partner, area))
        def _():
            act(own_copy(t, c))

    def relay_step(t, c, offset, act):
        @pl.when(inside(offset))
        def _():
            @pl.when(needs(partner, member(offset)))
            def _():
                act(relay_copy(t, c, offset))

    def edge_step(t, c, low, act):
        @pl.when(has_low if low else has_high)
        def _():
            act((low_copy if low else high_copy)(t, c))

    def go(copy):
        copy.start()

    def sent(copy):
        copy.wait_send()

    def export_sent(t, c):
        for offset in far_first:
            column_step(t, c, offset, sent)
        own_step(t, c, sent)

    def send_export(t, c):
        own_step(t, c, go)
        for offset in far_first:
            column_step(t, c, offset, go)

    def edges_sent(t, c):
        edge_step(t, c, True, sent)
        edge_step(t, c, False, sent)

    def wait_edges(t, c):
        @pl.when(has_high)
        def _():
            low_copy(t, c).wait_recv()

        @pl.when(has_low)
        def _():
            high_copy(t, c).wait_recv()

    def relay(t, c, offset):
        @pl.when(inside(offset))
        def _():
            @pl.when(needs(partner, member(offset)))
            def _():
                arrival(t, c, member(offset)).wait_recv()
                if t > 0:
                    relay_copy(t - 1, c, offset).wait_send()
                relay_copy(t, c, offset).start()

    def wait_far(t, c):
        @pl.when(needs(area, partner))
        def _():
            arrival(t, c, partner).wait_recv()

        for offset in near_first:
            @pl.when(inside(offset))
            def _(offset=offset):
                column, across = member(offset), partner + 2 * offset
                direct = jnp.logical_not(needs(partner, column))

                @pl.when(jnp.logical_and(direct, needs(area, column)))
                def _():
                    arrival(t, c, column).wait_recv()

                @pl.when(needs(area, across))
                def _():
                    arrival(t, c, across).wait_recv()

    def chain(pieces, w_of):
        total = None
        for k in range(0, len(pieces), 2):
            pair = jnp.concatenate([p() for p in pieces[k : k + 2]], axis=1)
            term = jnp.dot(pair, w_of(k, pair.shape[1]), preferred_element_type=jnp.float32)
            total = term if total is None else total + term
        return total

    def near_row(buffer, r, rows_of):
        pieces = [lambda k=k: buffer[near_idx[r, k]] for k in range(k_near)]
        total = chain(pieces, lambda k, n: weights[r, pl.ds(k * blk, n), :])
        acc[r, rows_of, :] = total + drive[r, rows_of, :].astype(jnp.float32)

    def far_row(t, c, r):
        pieces = [lambda k=k: fars[t, c][far_idx[r, k]] for k in range(k_far)]
        total = chain(pieces, lambda k, n: weights[r, pl.ds((k_near + k) * blk, n), :])
        current = acc[r, span(c), :] + total
        rates = start[r + 1, span(c), :] if t == 0 else nears[t, c][r + 1]
        leak = leak_ref[r]
        value = ((1.0 - leak) * rates.astype(jnp.float32) + leak * jnp.tanh(current)).astype(
            jnp.bfloat16
        )
        if t + 1 < STEPS:
            nears[t + 1, c][r + 1] = value
        else:
            out_ref[span(c), pl.ds(pl.multiple_of(r * blk, blk), blk)] = value

    def near_start(piece):
        count = rows // PIECES
        if piece == FIRST:
            wait_edges(0, 0)

        @pl.loop(piece * count, (piece + 1) * count, unroll=count)
        def _(r):
            near_row(start, r, slice(None))

    def near_chunk(t, c):
        wait_edges(t, c)

        @pl.loop(0, rows, unroll=rows)
        def _(r):
            near_row(nears[t, c], r, span(c))

    def far_first_row(t, c):
        if (t, c) == (0, 0):
            load_last()
        wait_far(t, c)
        if t + 1 == STEPS:
            @pl.loop(0, rows, unroll=rows)
            def _(r):
                far_row(t, c, r)

            return
        export_sent(t, c)
        far_row(t, c, 0)
        send_export(t + 1, c)

    def far_rest(t, c):
        if t > 0 or c == 0:
            edges_sent(t, c)
        edge_step(t + 1, c, True, go)

        @pl.loop(1, rows, unroll=rows - 1)
        def _(r):
            far_row(t, c, r)

        edge_step(t + 1, c, False, go)

    def send_down():
        load(0, 6).wait()
        for d in range(n_col - 1, 0, -1):
            column_step(0, 0, -d, go)

        @pl.when(side == 1)
        def _():
            for c in chunks:
                own_step(0, c, go)

        edge_step(0, 0, True, go)

    def send_high():
        load(rows - 1, 7).wait()

        @pl.when(has_high)
        def _():
            pl.semaphore_wait(in_sem.at[in_t], 1)

        edge_step(0, 0, False, go)

    def send_across():
        @pl.when(side == 0)
        def _():
            pl.semaphore_wait(in_sem.at[in_x], 1)
            for c in chunks:
                own_step(0, c, go)

    def send_up(d):
        @pl.when(inside(d))
        def _():
            pl.semaphore_wait(in_sem.at[d], 1)

        column_step(0, 0, d, go)

    def send_late(c):
        for offset in far_first:
            column_step(0, c, offset, go)

    def load_rest():
        zeros = jnp.zeros((part, blk), jnp.bfloat16)

        @pl.when(jnp.logical_not(has_low))
        def _():
            start[0] = jnp.zeros((batch, blk), jnp.bfloat16)
            for key in nears:
                nears[key][0] = zeros

        @pl.when(jnp.logical_not(has_high))
        def _():
            start[rows + 1] = jnp.zeros((batch, blk), jnp.bfloat16)
            for key in nears:
                nears[key][rows + 1] = zeros

        inner = start.at[pl.ds(2, rows - 2)]
        pltpu.make_async_copy(inner, inner, load_sem.at[0]).wait()
        load_near.wait()
        near_weights = weights.at[:, near_part]
        pltpu.make_async_copy(near_weights, near_weights, load_sem.at[1]).wait()
        pltpu.make_async_copy(drive, drive, load_sem.at[2]).wait()

    def load_last():
        far_weights = weights.at[:, far_part]
        pltpu.make_async_copy(far_weights, far_weights, load_sem.at[8]).wait()
        load_far.wait()
        load_leak.wait()

    steps = {
        "down": send_down,
        "across": send_across,
        "high": send_high,
        "up": send_up,
        "load": load_rest,
        "fetch": fetch,
        "late": send_late,
        "start": near_start,
        "first": far_first_row,
        "rest": far_rest,
        "near": near_chunk,
    }
    for name, *at in ORDER:
        if name == "up" and at[0] >= LONG:
            for d in range(LONG, n_col):
                send_up(d)
        elif name == "up":
            if at[0] < n_col:
                send_up(*at)
        elif name == "relay":
            t, c, offset = at
            away = abs(offset)
            if away >= LONG:
                for d in range(LONG, n_col):
                    relay(t, c, d if offset > 0 else -d)
            elif away < n_col:
                relay(t, c, offset)
        else:
            steps[name](*at)

    t = STEPS - 1
    for c in chunks:
        export_sent(t, c)
        for offset in near_first:
            relay_step(t, c, offset, sent)
        edges_sent(t, c)


def body(n_area, n_tile, start_rates, stim_drive, leak_rates, block_weights, near_index, far_index):
    _, batch, width = start_rates.shape
    _, rows, slots, blk, _ = block_weights.shape
    k_near, k_far = near_index.shape[-1], far_index.shape[-1]
    sizes = (n_area, n_tile, batch, rows, k_near, k_far, blk)
    part = batch // CHUNKS
    any_spec = pl.BlockSpec(memory_space=pl.ANY)
    vmem_spec = pl.BlockSpec(memory_space=pltpu.VMEM)
    scratch = (
        [
            pltpu.SMEM((rows, k_near), jnp.int32),
            pltpu.SMEM((rows, k_far), jnp.int32),
            pltpu.VMEM((rows, 1, blk), jnp.float32),
            pltpu.VMEM((rows, batch, blk), jnp.bfloat16),
            pltpu.VMEM((rows, slots * blk, blk), jnp.bfloat16),
            pltpu.VMEM((rows, batch, blk), jnp.float32),
            pltpu.VMEM((rows + 2, batch, blk), jnp.bfloat16),
        ]
        + [pltpu.VMEM((rows + 2, part, blk), jnp.bfloat16) for _ in range((STEPS - 1) * CHUNKS)]
        + [pltpu.VMEM((n_area, part, blk), jnp.bfloat16) for _ in range(STEPS * CHUNKS)]
    )
    out = pl.pallas_call(
        functools.partial(kernel, sizes),
        out_shape=pltpu.MemorySpace.VMEM((batch, width), jnp.bfloat16),
        in_specs=[any_spec] * 6,
        out_specs=vmem_spec,
        scratch_shapes=scratch,
        compiler_params=pltpu.CompilerParams(
            collective_id=0, has_side_effects=True, vmem_limit_bytes=56 * 1024 * 1024
        ),
        name="rate_steps",
    )(
        near_index[0],
        far_index[0],
        start_rates[0],
        stim_drive[0],
        leak_rates[0].reshape(rows, 1, blk),
        block_weights[0].reshape(rows, slots * blk, blk),
    )
    return out[None]


def solution(mesh):
    in_specs = (
        P("area", None, "tile"),
        P("area", None, "tile"),
        P("area", "tile"),
        P("area", "tile", None, None, None),
        P("area", "tile", None),
        P("area", "tile", None),
    )
    out_specs = P("area", None, "tile")
    local = functools.partial(body, mesh.shape["area"], mesh.shape["tile"])
    return jax.shard_map(local, mesh=mesh, in_specs=in_specs, out_specs=out_specs, check_vma=False)
```
